32 devices in a mesh: branch: 2 (over x), sample: 16 (over z, y, core).
Axes of the slice: x: 2, y: 2, z: 4, core: 2. Of those that a mesh axis runs over, the one named last changes fastest.
Arguments:
- abundance: bfloat16 [128, 32768], P('sample', 'branch'), may hold values from 0.01 to 100, as said below
- length_table: float32 [32768], P('branch'), may hold values from 0.01 to 1, as said below
- branch_rows: int32 [32768], P('branch'), may hold values from 0 to 16383, as said below
Outputs:
- distance: float32 [128, 128], P('sample', 'branch')
The draws below stay inside these ranges and needn't reach their ends.
Inputs may be any that keep to these rules, and one draw needn't show every extreme that they name: `abundance`: entries are positive. `length_table`: positive branch lengths. `branch_rows`: within each aligned block of 16384 entries every number from 0 to 16383 appears once.
All inputs are finite; a program needn't handle non-finite values.
Results may differ from the reference program's by a relative error of at most 0.0003.
Values may be sent and summed in bfloat16 or wider, within the bound.
A program may use at most 64 MiB of HBM per device.

```python
import jax
import jax.numpy as jnp
from jax import lax

BRANCHES = 32768
SAMPLES = 128
N_BRANCH = 2


def group_width():
    return max(min(256, BRANCHES // 64), 1)


def group_lengths(key):
    group_count = BRANCHES // group_width()
    length_key = jax.random.fold_in(key, 31)
    return jnp.exp(jax.random.uniform(length_key, (group_count,), jnp.float32, jnp.log(0.02), jnp.log(0.5)))


def row_orders(key):
    per_group = BRANCHES // N_BRANCH
    keys = jax.random.split(jax.random.fold_in(key, 21), N_BRANCH)
    orders = jax.vmap(lambda single: jax.random.permutation(single, per_group))(keys)
    return orders.reshape(-1).astype(jnp.int32)


def draw_abundance(key, part):
    width = group_width()
    group_count = BRANCHES // width
    spans = group_lengths(key)
    level = (jnp.log(spans) - jnp.log(0.02)) / jnp.log(25.0)
    spread = jnp.log(100.0) * (1.0 - level) + jnp.log(2.0) * level
    scale_key = jax.random.fold_in(key, 11)
    value_key = jax.random.fold_in(key, 12)
    unit = jax.random.uniform(scale_key, (SAMPLES, group_count), jnp.float32, 0.0, 1.0)
    scales = jnp.exp(unit * spread[None, :])
    scales = jnp.repeat(scales, width, axis=1)
    base = jnp.exp(jax.random.uniform(value_key, (SAMPLES, BRANCHES), jnp.float32, jnp.log(0.01), 0.0))
    rising = 3.0 ** (jnp.arange(BRANCHES, dtype=jnp.float32) / BRANCHES)
    result = jnp.clip(base * scales * rising[None, :], 0.01, 100.0)
    return result.astype(jnp.bfloat16)


def draw_length_table(key, part):
    width = group_width()
    spans = jnp.repeat(group_lengths(key), width)
    rough_key = jax.random.fold_in(key, 41)
    rough = jnp.exp(jax.random.uniform(rough_key, (BRANCHES,), jnp.float32, jnp.log(0.5), jnp.log(2.0)))
    per_branch = jnp.clip(spans * rough, 0.01, 1.0)
    per_group = BRANCHES // N_BRANCH
    offsets = jnp.arange(BRANCHES, dtype=jnp.int32) // per_group * per_group
    places = (offsets + row_orders(key)).astype(jnp.int32)
    table = jnp.zeros((BRANCHES,), jnp.float32).at[places].set(per_branch)
    return table.astype(jnp.float32)


def draw_branch_rows(key, part):
    return row_orders(key)


def setup_inputs(seed: int = 0) -> dict:
    key_of = jax.random.split(jax.random.key(seed), 4)
    return {
        "abundance": draw_abundance(jax.random.fold_in(key_of[3], 71), 0),
        "length_table": draw_length_table(jax.random.fold_in(key_of[3], 71), 0),
        "branch_rows": draw_branch_rows(jax.random.fold_in(key_of[3], 71), 0),
    }


def reference(abundance, length_table, branch_rows):
    values = abundance.astype(jnp.float32)
    totals = lax.optimization_barrier(jnp.sum(values, axis=1))
    shares = (values / totals[:, None]).astype(jnp.bfloat16)
    per_group = BRANCHES // N_BRANCH
    offsets = jnp.arange(BRANCHES, dtype=jnp.int32) // per_group * per_group
    lengths = length_table[(offsets + branch_rows).astype(jnp.int32)]
    columns = shares.T
    block_size = 128
    block_count = BRANCHES // block_size

    def row_block(index):
        mine = lax.dynamic_slice_in_dim(columns, (index * 16).astype(jnp.int32), 16, 1)

        def absorb(carry, turn):
            begin = (turn * block_size).astype(jnp.int32)
            left = lax.dynamic_slice_in_dim(mine, begin, block_size, 0).astype(jnp.float32)[:, :, None]
            right = lax.dynamic_slice_in_dim(columns, begin, block_size, 0).astype(jnp.float32)[:, None, :]
            weight = lax.dynamic_slice_in_dim(lengths, begin, block_size, 0)[:, None, None]
            summed = left + right
            inverse = lax.rsqrt(summed)
            return ((carry[0] + lax.optimization_barrier(jnp.sum(weight * jnp.abs(left - right) * inverse, axis=0)), carry[1] + lax.optimization_barrier(jnp.sum(weight * summed * inverse, axis=0))), None)
        empty = jnp.zeros((16, SAMPLES), jnp.float32)
        result, unused = lax.scan(absorb, (empty, empty), jnp.arange(block_count, dtype=jnp.int32))
        return result
    numer, denom = lax.map(row_block, jnp.arange(SAMPLES // 16, dtype=jnp.int32))
    numer = numer.reshape(SAMPLES, SAMPLES)
    denom = denom.reshape(SAMPLES, SAMPLES)
    return numer / denom
```

```python
import functools

import jax
import jax.numpy as jnp
from jax import lax
from jax.experimental import pallas as pl
from jax.experimental.pallas import tpu as pltpu
from jax.sharding import PartitionSpec as P

MESH = pl.DeviceIdType.MESH
F32 = jnp.float32
ROWS = 8
LANES = 128


def pair_sums(mine, other, lengths):
    count, width = mine.shape
    others = other.shape[0]
    block_size = width
    while block_size > 512 and block_size % 2 == 0 and (block_size * count * others > 2097152):
        block_size = block_size // 2
    block_count = width // block_size

    def absorb(carry, turn):
        begin = turn * block_size
        left = lax.dynamic_slice_in_dim(mine, begin, block_size, 1).astype(F32)[:, None, :]
        right = lax.dynamic_slice_in_dim(other, begin, block_size, 1).astype(F32)[None, :, :]
        weight = lax.dynamic_slice_in_dim(lengths, begin, block_size, 0)[None, None, :]
        summed = left + right
        inverse = lax.rsqrt(summed)
        return (
            (
                carry[0] + jnp.sum(weight * jnp.abs(left - right) * inverse, axis=2),
                carry[1] + jnp.sum(weight * summed * inverse, axis=2),
            ),
            None,
        )

    empty = jnp.zeros((count, others), F32)
    result, unused = lax.scan(absorb, (empty, empty), jnp.arange(block_count, dtype=jnp.int32))
    return result


def plain_body(abundance, length_table, branch_rows):
    values = abundance.astype(F32)
    totals = lax.psum(jnp.sum(values, axis=1), "branch")
    shares = (values / totals[:, None]).astype(jnp.bfloat16)
    lengths = jnp.take(length_table, branch_rows)
    numer_part, denom_part = pair_sums(
        shares, lax.all_gather(shares, "sample", axis=0, tiled=True), lengths
    )
    summed = (
        lax.psum_scatter(numer_part, "branch", scatter_dimension=1, tiled=True),
        lax.psum_scatter(denom_part, "branch", scatter_dimension=1, tiled=True),
    )
    return summed[0] / summed[1]


def kernel(
    axes, n_branch, n_sample, chunk,
    ab_hbm, table_hbm, rows_hbm, out_ref,
    ab, table, rows, x_buf, tot_send, tot_buf, inv_ref, p_ref, l2_ref, mask_ref, cell, done, res_buf,
    local_sem, own_sem, x_send_sem, x_recv_sem, t_send_sem, t_recv_sem, r_send_sem, r_recv_sem,
):
    n_dev = n_branch * n_sample
    depth = chunk // LANES
    part = n_sample // n_branch
    half = part * ROWS
    group = part // 2
    my_t = lax.axis_index("branch")
    my_s = lax.axis_index("sample")
    me = my_t * n_sample + my_s
    my_side, my_low = my_s // part, lax.rem(my_s, part)

    def place(t, s):
        where = {"branch": t, "sample": s}
        return tuple(where[name] for name in axes)

    def peer_at(k):
        flat = lax.bitwise_xor(me, k)
        return flat, flat // n_sample, lax.rem(flat, n_sample)

    barrier = pltpu.get_barrier_semaphore()

    def greet(k, carry):
        flat, t, s = peer_at(n_dev - k)
        pl.semaphore_signal(barrier, inc=1, device_id=place(t, s), device_id_type=MESH)
        return carry

    ab_copy = pltpu.make_async_copy(ab_hbm, ab, local_sem.at[0])
    table_copy = pltpu.make_async_copy(table_hbm, table, local_sem.at[1])
    rows_copy = pltpu.make_async_copy(rows_hbm.at[my_s], rows, local_sem.at[2])
    own_copy = pltpu.make_async_copy(
        ab_hbm.at[:, pl.ds(pl.multiple_of(my_s * chunk, chunk), chunk)], x_buf.at[my_s], own_sem
    )
    ab_copy.start()
    lax.fori_loop(1, n_dev, greet, 0)
    table_copy.start()
    rows_copy.start()
    own_copy.start()

    def x_copy(to_s, slot, recv):
        return pltpu.make_async_remote_copy(
            src_ref=ab_hbm.at[:, pl.ds(pl.multiple_of(to_s * chunk, chunk), chunk)],
            dst_ref=x_buf.at[slot],
            send_sem=x_send_sem.at[to_s],
            recv_sem=x_recv_sem.at[recv],
            device_id=place(my_t, to_s),
            device_id_type=MESH,
        )

    def t_copy(flat, t, s, slot):
        return pltpu.make_async_remote_copy(
            src_ref=tot_send,
            dst_ref=tot_buf.at[slot],
            send_sem=t_send_sem.at[flat],
            recv_sem=t_recv_sem.at[slot],
            device_id=place(t, s),
            device_id_type=MESH,
        )

    def r_copy(source, flat, t, s, slot):
        return pltpu.make_async_remote_copy(
            src_ref=source,
            dst_ref=res_buf.at[slot],
            send_sem=r_send_sem.at[flat],
            recv_sem=r_recv_sem.at[slot],
            device_id=place(t, s),
            device_id_type=MESH,
        )

    lane = lax.broadcasted_iota(jnp.int32, (ROWS, LANES), 1)
    sub = lax.broadcasted_iota(jnp.int32, (ROWS, LANES), 0)
    eye = lane == sub
    column = lane % half
    is_numer = lane < half

    cell[...] = jnp.zeros_like(cell)
    ab_copy.wait()
    step = min(chunk, 1024)

    def add_up(turn, acc):
        return acc + ab[:, pl.ds(pl.multiple_of(turn * step, step), step)].astype(F32)

    acc = lax.fori_loop(0, n_sample * chunk // step, add_up, jnp.zeros((ROWS, step), F32))
    total = jnp.sum(acc, axis=1, keepdims=True)
    line = jnp.sum(jnp.where(eye, total, 0.0), axis=0, keepdims=True)
    tot_send[...] = line
    tot_buf[me] = line

    pl.semaphore_wait(barrier, n_dev - 1)

    def send_t(k):
        flat, t, s = peer_at(k)
        t_copy(flat, t, s, me).start()

    def send_x(k):
        x_copy(lax.bitwise_xor(my_s, k), my_s, my_s).start()

    send_t(n_sample)
    for k in range(1, group):
        send_t(k)
        send_t(n_sample + k)
        send_x(k)
    for k in range(group, n_sample):
        send_t(k)
        send_t(n_sample + k)
    for k in range(group):
        send_x(part + k)
        send_x(group + k)
    for k in range(part + group, n_sample):
        send_x(k)

    table_copy.wait()
    rows_copy.wait()
    index = rows[...]
    high, low = index // LANES, index % LANES

    def look_up(h, found):
        line = jnp.broadcast_to(table[pl.ds(h, 1), :], (depth, LANES))
        picked = jnp.take_along_axis(line, low, axis=1, mode="promise_in_bounds")
        return jnp.where(high == h, picked, found)

    lengths = lax.fori_loop(
        0, table.shape[0], look_up, jnp.zeros((depth, LANES), F32), unroll=8
    )
    l2_ref[...] = lengths * lengths

    wide = (half, LANES)
    row_at = lax.broadcasted_iota(jnp.int32, wide, 0)
    column_at = lax.broadcasted_iota(jnp.int32, wide, 1) % half
    row_block = lax.bitwise_xor(row_at // ROWS, my_low)
    column_block = lax.bitwise_xor(column_at // ROWS, my_low)
    apart = (column_block - row_block + part) % group
    turned = (2 * apart < group) | ((2 * apart == group) & (2 * (row_block % group) < group))
    inside = (row_at - column_at + half) % ROWS
    same = row_block == column_block
    row_half, column_half = row_block // group, column_block // group
    direct = (
        (same & (2 * inside <= ROWS))
        | (~same & (row_half == column_half) & turned)
        | (row_half > column_half)
    )
    mask_ref[...] = jnp.where(same & (inside == 0), 2, jnp.where(direct, 1, 0))

    def columns_of(k):
        s = lax.bitwise_xor(my_s, k)
        total = tot_buf[s]
        for t in range(1, n_branch):
            total = total + tot_buf[t * n_sample + s]
        spread = jnp.where(eye, jnp.broadcast_to(total, (ROWS, LANES)), 0.0)
        return 1.0 / jnp.broadcast_to(jnp.sum(spread, axis=1, keepdims=True), (ROWS, LANES))

    def await_t(k, carry):
        s = lax.bitwise_xor(my_s, k)
        for t in range(n_branch):
            flat = t * n_sample + s

            @pl.when(flat != me)
            def _():
                t_copy(flat, t, s, flat).wait()

        return carry

    def await_x(k, carry):
        s = lax.bitwise_xor(my_s, k)
        x_copy(s, s, s).wait()
        return carry

    def prepare(k):
        s = lax.bitwise_xor(my_s, k)
        inverse = inv_ref[k]
        for r in range(depth):
            values = x_buf[s, :, r * LANES:(r + 1) * LANES].astype(F32)
            shares = (values * inverse).astype(jnp.bfloat16).astype(F32)
            p_ref[k, r] = shares * l2_ref[r:r + 1, :]

    def low_of(k):
        return lax.bitwise_xor(my_low, lax.rem(k, part))

    def terms(p, q):
        summed = p + q
        inverse = lax.rsqrt(summed)
        return jnp.maximum(p, q) * inverse, summed * inverse

    def gather(pieces):
        top, bottom = pieces[0]
        for more_top, more_bottom in pieces[1:]:
            top, bottom = top + more_top, bottom + more_bottom
        return top, bottom

    def pairs(j_block, i_block):
        others = [p_ref[j_block, r] for r in range(depth)]
        sums = []
        for i in range(ROWS):
            sums += gather(
                [terms(p_ref[i_block, r, pl.ds(i, 1), :], others[r]) for r in range(depth)]
            )
        return tuple(sums)

    def place_pairs(at, i_block, sums):
        base = low_of(i_block) * ROWS
        now = cell[at]
        for i in range(ROWS):
            top = jnp.sum(sums[2 * i], axis=1, keepdims=True)
            bottom = jnp.sum(sums[2 * i + 1], axis=1, keepdims=True)
            now = jnp.where(column == base + i, jnp.where(is_numer, top, bottom), now)
        cell[at] = now

    def own_pairs(block):
        mine = [p_ref[block, r] for r in range(depth)]
        sums = []
        for turn in range(1, ROWS // 2 + 1):
            sums += gather([terms(pltpu.roll(q, turn, 0), q) for q in mine])
        return tuple(sums)

    def place_own(at, block, sums):
        base = low_of(block) * ROWS
        now = cell[at]
        for turn in range(1, ROWS // 2 + 1):
            top = jnp.sum(sums[2 * turn - 2], axis=1, keepdims=True)
            bottom = jnp.sum(sums[2 * turn - 1], axis=1, keepdims=True)
            here = column - base == (sub + ROWS - turn) % ROWS
            now = jnp.where(here, jnp.where(is_numer, top, bottom), now)
        cell[at] = now

    def cell_of(k):
        return (k // part) * part + low_of(k)

    def work_through(items, waiting=None):
        for item in items:
            if len(item) == 1:
                sums = own_pairs(item[0])
                later = functools.partial(place_own, cell_of(item[0]), item[0], sums)
            else:
                at, j_block, i_block = item
                sums = pairs(j_block, i_block)
                later = functools.partial(place_pairs, at, i_block, sums)
            if waiting is not None:
                waiting()
            waiting = later
        return waiting

    def within(base):
        found = [(base + j,) for j in range(group)]
        for turn in range(1, group // 2 + 1):
            for j in range(group if 2 * turn < group else group // 2):
                found.append((cell_of(jnp.int32(base + j)), base + j, base + (j + turn) % group))
        return found

    def between(j_base, i_base):
        return [
            (cell_of(jnp.int32(j_base + j)), j_base + j, i_base + i)
            for j in range(group)
            for i in range(group)
        ]

    def deliver(source, t, s, may_be_me=False):
        flat = t * n_sample + s
        copy = r_copy(source, flat, t, s, me)
        if not may_be_me:
            copy.start()
            return

        @pl.when(flat != me)
        def _():
            copy.start()

        @pl.when(flat == me)
        def _():
            res_buf[me] = source[...]

    def mirrored(start):
        whole = cell[start:start + part].reshape(half, LANES)
        square = jnp.concatenate([whole, pltpu.roll(whole, half, 1)], axis=0)
        return whole, square.T[:half]

    def settle(start):
        whole, turned = mirrored(start)
        mask = mask_ref[...]
        first = lax.broadcasted_iota(jnp.int32, wide, 1) < half
        fixed = jnp.where(first, 0.5, 1.0)
        full = jnp.where(mask == 1, whole, jnp.where(mask == 2, fixed, turned))
        done[start:start + part] = full.reshape(part, ROWS, LANES)

    def cross(base, late):
        per = 2

        def rows_of(turn, carry):
            if late:
                for u in range(per):
                    await_x(base + turn * per + u, 0)
                for u in range(per):
                    prepare(base + turn * per + u)
            waiting = None
            for u in range(per):
                j_block = base + turn * per + u
                at = n_sample + low_of(j_block)
                waiting = work_through([(at, j_block, i) for i in range(part)], waiting)
            waiting()
            for u in range(per):
                s = lax.bitwise_xor(my_s, base + turn * per + u)
                deliver(cell.at[n_sample + lax.rem(s, part)], my_side, s)
            return carry

        lax.fori_loop(0, group // per, rows_of, 0)

    lax.fori_loop(0, group, await_t, 0)
    for k in range(group):
        inv_ref[k] = columns_of(k)
    own_copy.wait()
    lax.fori_loop(1, group, await_x, 0)
    for k in range(group):
        prepare(k)
    work_through(within(0))()
    lax.fori_loop(group, n_sample, await_t, 0)
    for k in range(group, n_sample):
        inv_ref[k] = columns_of(k)
    lax.fori_loop(group, part, await_x, 0)
    for k in range(group, part):
        prepare(k)
    work_through(within(group) + between(group, 0))()
    settle(0)
    for k in range(part - 1, -1, -1):
        s = lax.bitwise_xor(my_s, k)
        deliver(done.at[lax.rem(s, part)], my_side, s, k == 0)
    cross(part, True)
    work_through(within(part))()
    lax.fori_loop(part + group, n_sample, await_x, 0)
    for k in range(part + group, n_sample):
        prepare(k)
    work_through(within(part + group) + between(part + group, part))()
    settle(part)
    for k in range(n_sample - 1, part - 1, -1):
        s = lax.bitwise_xor(my_s, k)
        deliver(done.at[part + lax.rem(s, part)], 1 - my_side, s)
    cross(part + group, False)
    done[n_sample:n_sample + part] = mirrored(n_sample)[1].reshape(part, ROWS, LANES)
    for k in range(part - 1, -1, -1):
        s = lax.bitwise_xor(my_s, k)
        deliver(done.at[n_sample + lax.rem(s, part)], 1 - my_side, s, k == 0)

    def await_r(k, carry):
        flat, t, s = peer_at(k)
        r_copy(done.at[0], flat, t, s, flat).wait()
        return carry

    lax.fori_loop(1, n_dev, await_r, 0)
    parts = [res_buf[k] for k in range(n_dev)]
    while len(parts) > 1:
        parts = [x + y for x, y in zip(parts[::2], parts[1::2])]
    out_ref[...] = parts[0]


def kernel_body(axes, n_branch, n_sample, abundance, length_table, branch_rows):
    width = abundance.shape[1]
    chunk = width // n_sample
    depth = chunk // LANES
    n_dev = n_branch * n_sample
    half = n_sample * ROWS // n_branch
    sums = pl.pallas_call(
        functools.partial(kernel, axes, n_branch, n_sample, chunk),
        out_shape=pltpu.VMEM((ROWS, LANES), F32),
        in_specs=[pl.BlockSpec(memory_space=pl.ANY)] * 3,
        out_specs=pl.BlockSpec(memory_space=pltpu.VMEM),
        scratch_shapes=[
            pltpu.VMEM((ROWS, width), jnp.bfloat16),
            pltpu.VMEM((width // LANES, LANES), F32),
            pltpu.VMEM((depth, LANES), jnp.int32),
            pltpu.VMEM((n_sample, ROWS, chunk), jnp.bfloat16),
            pltpu.VMEM((1, LANES), F32),
            pltpu.VMEM((n_dev, 1, LANES), F32),
            pltpu.VMEM((n_sample, ROWS, LANES), F32),
            pltpu.VMEM((n_sample, depth, ROWS, LANES), F32),
            pltpu.VMEM((depth, LANES), F32),
            pltpu.VMEM((half, LANES), jnp.int32),
            pltpu.VMEM((n_sample + half // ROWS, ROWS, LANES), F32),
            pltpu.VMEM((n_sample + half // ROWS, ROWS, LANES), F32),
            pltpu.VMEM((n_dev, ROWS, LANES), F32),
            pltpu.SemaphoreType.DMA((3,)),
            pltpu.SemaphoreType.DMA,
            pltpu.SemaphoreType.DMA((n_sample,)),
            pltpu.SemaphoreType.DMA((n_sample,)),
            pltpu.SemaphoreType.DMA((n_dev,)),
            pltpu.SemaphoreType.DMA((n_dev,)),
            pltpu.SemaphoreType.DMA((n_dev,)),
            pltpu.SemaphoreType.DMA((n_dev,)),
        ],
        compiler_params=pltpu.CompilerParams(collective_id=0, has_side_effects=True),
    )(
        abundance,
        length_table.reshape(width // LANES, LANES),
        branch_rows.reshape(n_sample, depth, LANES),
    )
    big, den = sums[:, :half], sums[:, half:2 * half]
    return (2.0 * big - den) / den


def solution(mesh):
    n_branch, n_sample = mesh.shape["branch"], mesh.shape["sample"]
    axes = tuple(mesh.axis_names)

    def body(abundance, length_table, branch_rows):
        rows, width = abundance.shape
        fits = (
            rows == ROWS
            and n_sample * ROWS == LANES
            and n_branch == 2
            and width % (n_sample * ROWS * LANES) == 0
        )
        if not fits:
            return plain_body(abundance, length_table, branch_rows)
        return kernel_body(axes, n_branch, n_sample, abundance, length_table, branch_rows)

    placed = (P("sample", "branch"), P("branch"), P("branch"))
    return jax.shard_map(
        body, mesh=mesh, in_specs=placed, out_specs=P("sample", "branch"), check_vma=False
    )
```

```python
import functools

import jax
import jax.numpy as jnp
from jax import lax
from jax.experimental import pallas as pl
from jax.experimental.pallas import tpu as pltpu
from jax.sharding import PartitionSpec as P

MESH = pl.DeviceIdType.MESH
F32 = jnp.float32
ROWS = 8
LANES = 128


def pair_sums(mine, other, lengths):
    count, width = mine.shape
    others = other.shape[0]
    block_size = width
    while block_size > 512 and block_size % 2 == 0 and (block_size * count * others > 2097152):
        block_size = block_size // 2
    block_count = width // block_size

    def absorb(carry, turn):
        begin = turn * block_size
        left = lax.dynamic_slice_in_dim(mine, begin, block_size, 1).astype(F32)[:, None, :]
        right = lax.dynamic_slice_in_dim(other, begin, block_size, 1).astype(F32)[None, :, :]
        weight = lax.dynamic_slice_in_dim(lengths, begin, block_size, 0)[None, None, :]
        summed = left + right
        inverse = lax.rsqrt(summed)
        return (
            (
                carry[0] + jnp.sum(weight * jnp.abs(left - right) * inverse, axis=2),
                carry[1] + jnp.sum(weight * summed * inverse, axis=2),
            ),
            None,
        )

    empty = jnp.zeros((count, others), F32)
    result, unused = lax.scan(absorb, (empty, empty), jnp.arange(block_count, dtype=jnp.int32))
    return result


def plain_body(abundance, length_table, branch_rows):
    values = abundance.astype(F32)
    totals = lax.psum(jnp.sum(values, axis=1), "branch")
    shares = (values / totals[:, None]).astype(jnp.bfloat16)
    lengths = jnp.take(length_table, branch_rows)
    numer_part, denom_part = pair_sums(
        shares, lax.all_gather(shares, "sample", axis=0, tiled=True), lengths
    )
    summed = (
        lax.psum_scatter(numer_part, "branch", scatter_dimension=1, tiled=True),
        lax.psum_scatter(denom_part, "branch", scatter_dimension=1, tiled=True),
    )
    return summed[0] / summed[1]


def kernel(
    axes, n_branch, n_sample, chunk,
    ab_hbm, table_hbm, rows_hbm, out_ref,
    ab, table, rows, x_buf, tot_send, tot_buf, inv_ref, p_ref, l2_ref, mask_ref, cell, done, res_buf,
    local_sem, own_sem, x_send_sem, x_recv_sem, t_send_sem, t_recv_sem, r_send_sem, r_recv_sem,
):
    n_dev = n_branch * n_sample
    depth = chunk // LANES
    part = n_sample // n_branch
    half = part * ROWS
    group = part // 2
    my_t = lax.axis_index("branch")
    my_s = lax.axis_index("sample")
    me = my_t * n_sample + my_s
    my_side, my_low = my_s // part, lax.rem(my_s, part)

    def place(t, s):
        where = {"branch": t, "sample": s}
        return tuple(where[name] for name in axes)

    def peer_at(k):
        flat = lax.bitwise_xor(me, k)
        return flat, flat // n_sample, lax.rem(flat, n_sample)

    barrier = pltpu.get_barrier_semaphore()

    def greet(k, carry):
        flat, t, s = peer_at(n_dev - k)
        pl.semaphore_signal(barrier, inc=1, device_id=place(t, s), device_id_type=MESH)
        return carry

    ab_copy = pltpu.make_async_copy(ab_hbm, ab, local_sem.at[0])
    table_copy = pltpu.make_async_copy(table_hbm, table, local_sem.at[1])
    rows_copy = pltpu.make_async_copy(rows_hbm.at[my_s], rows, local_sem.at[2])
    own_copy = pltpu.make_async_copy(
        ab_hbm.at[:, pl.ds(pl.multiple_of(my_s * chunk, chunk), chunk)], x_buf.at[my_s], own_sem
    )
    ab_copy.start()
    lax.fori_loop(1, n_dev, greet, 0)
    table_copy.start()
    rows_copy.start()
    own_copy.start()

    def x_copy(to_s, slot, recv):
        return pltpu.make_async_remote_copy(
            src_ref=ab_hbm.at[:, pl.ds(pl.multiple_of(to_s * chunk, chunk), chunk)],
            dst_ref=x_buf.at[slot],
            send_sem=x_send_sem.at[to_s],
            recv_sem=x_recv_sem.at[recv],
            device_id=place(my_t, to_s),
            device_id_type=MESH,
        )

    def t_copy(flat, t, s, slot):
        return pltpu.make_async_remote_copy(
            src_ref=tot_send,
            dst_ref=tot_buf.at[slot],
            send_sem=t_send_sem.at[flat],
            recv_sem=t_recv_sem.at[slot],
            device_id=place(t, s),
            device_id_type=MESH,
        )

    def r_copy(source, flat, t, s, slot):
        return pltpu.make_async_remote_copy(
            src_ref=source,
            dst_ref=res_buf.at[slot],
            send_sem=r_send_sem.at[flat],
            recv_sem=r_recv_sem.at[slot],
            device_id=place(t, s),
            device_id_type=MESH,
        )

    lane = lax.broadcasted_iota(jnp.int32, (ROWS, LANES), 1)
    sub = lax.broadcasted_iota(jnp.int32, (ROWS, LANES), 0)
    eye = lane == sub
    column = lane % half
    is_numer = lane < half

    cell[...] = jnp.zeros_like(cell)
    ab_copy.wait()
    step = min(chunk, 1024)

    def add_up(turn, acc):
        return acc + ab[:, pl.ds(pl.multiple_of(turn * step, step), step)].astype(F32)

    acc = lax.fori_loop(0, n_sample * chunk // step, add_up, jnp.zeros((ROWS, step), F32))
    total = jnp.sum(acc, axis=1, keepdims=True)
    line = jnp.sum(jnp.where(eye, total, 0.0), axis=0, keepdims=True)
    tot_send[...] = line
    tot_buf[me] = line

    pl.semaphore_wait(barrier, n_dev - 1)

    def send_t(k):
        flat, t, s = peer_at(k)
        t_copy(flat, t, s, me).start()

    def send_x(k):
        x_copy(lax.bitwise_xor(my_s, k), my_s, my_s).start()

    send_t(n_sample)
    for k in range(1, group):
        send_t(k)
        send_t(n_sample + k)
        send_x(k)
    for k in range(group, n_sample):
        send_t(k)
        send_t(n_sample + k)
    early = (part + group - 2, part + group - 1)
    for k in (*range(group, part), *early, *range(part, part + group - 2)):
        send_x(k)
    for k in range(part + group, n_sample):
        send_x(k)

    table_copy.wait()
    rows_copy.wait()
    index = rows[...]
    high, low = index // LANES, index % LANES

    def look_up(h, found):
        line = jnp.broadcast_to(table[pl.ds(h, 1), :], (depth, LANES))
        picked = jnp.take_along_axis(line, low, axis=1, mode="promise_in_bounds")
        return jnp.where(high == h, picked, found)

    lengths = lax.fori_loop(
        0, table.shape[0], look_up, jnp.zeros((depth, LANES), F32), unroll=8
    )
    l2_ref[...] = lengths * lengths

    wide = (half, LANES)
    row_at = lax.broadcasted_iota(jnp.int32, wide, 0)
    column_at = lax.broadcasted_iota(jnp.int32, wide, 1) % half
    row_block = lax.bitwise_xor(row_at // ROWS, my_low)
    column_block = lax.bitwise_xor(column_at // ROWS, my_low)
    apart = (column_block - row_block + part) % group
    turned = (2 * apart < group) | ((2 * apart == group) & (2 * (row_block % group) < group))
    inside = (row_at - column_at + half) % ROWS
    same = row_block == column_block
    row_half, column_half = row_block // group, column_block // group
    direct = (
        (same & (2 * inside <= ROWS))
        | (~same & (row_half == column_half) & turned)
        | (row_half > column_half)
    )
    mask_ref[...] = jnp.where(same & (inside == 0), 2, jnp.where(direct, 1, 0))

    def columns_of(k):
        s = lax.bitwise_xor(my_s, k)
        total = tot_buf[s]
        for t in range(1, n_branch):
            total = total + tot_buf[t * n_sample + s]
        spread = jnp.where(eye, jnp.broadcast_to(total, (ROWS, LANES)), 0.0)
        return 1.0 / jnp.broadcast_to(jnp.sum(spread, axis=1, keepdims=True), (ROWS, LANES))

    def await_t(k, carry):
        s = lax.bitwise_xor(my_s, k)
        for t in range(n_branch):
            flat = t * n_sample + s

            @pl.when(flat != me)
            def _():
                t_copy(flat, t, s, flat).wait()

        return carry

    def await_x(k, carry):
        s = lax.bitwise_xor(my_s, k)
        x_copy(s, s, s).wait()
        return carry

    def prepare(k):
        s = lax.bitwise_xor(my_s, k)
        inverse = inv_ref[k]
        for r in range(depth):
            values = x_buf[s, :, r * LANES:(r + 1) * LANES].astype(F32)
            shares = (values * inverse).astype(jnp.bfloat16).astype(F32)
            p_ref[k, r] = shares * l2_ref[r:r + 1, :]

    def low_of(k):
        return lax.bitwise_xor(my_low, lax.rem(k, part))

    def terms(p, q):
        summed = p + q
        inverse = lax.rsqrt(summed)
        return jnp.maximum(p, q) * inverse, summed * inverse

    def gather(pieces):
        top, bottom = pieces[0]
        for more_top, more_bottom in pieces[1:]:
            top, bottom = top + more_top, bottom + more_bottom
        return top, bottom

    def pairs(j_block, i_block):
        others = [p_ref[j_block, r] for r in range(depth)]
        sums = []
        for i in range(ROWS):
            sums += gather(
                [terms(p_ref[i_block, r, pl.ds(i, 1), :], others[r]) for r in range(depth)]
            )
        return tuple(sums)

    def place_pairs(at, i_block, sums):
        base = low_of(i_block) * ROWS
        now = cell[at]
        for i in range(ROWS):
            top = jnp.sum(sums[2 * i], axis=1, keepdims=True)
            bottom = jnp.sum(sums[2 * i + 1], axis=1, keepdims=True)
            now = jnp.where(column == base + i, jnp.where(is_numer, top, bottom), now)
        cell[at] = now

    def own_pairs(block):
        mine = [p_ref[block, r] for r in range(depth)]
        sums = []
        for turn in range(1, ROWS // 2 + 1):
            sums += gather([terms(pltpu.roll(q, turn, 0), q) for q in mine])
        return tuple(sums)

    def place_own(at, block, sums):
        base = low_of(block) * ROWS
        now = cell[at]
        for turn in range(1, ROWS // 2 + 1):
            top = jnp.sum(sums[2 * turn - 2], axis=1, keepdims=True)
            bottom = jnp.sum(sums[2 * turn - 1], axis=1, keepdims=True)
            here = column - base == (sub + ROWS - turn) % ROWS
            now = jnp.where(here, jnp.where(is_numer, top, bottom), now)
        cell[at] = now

    def cell_of(k):
        return (k // part) * part + low_of(k)

    def work_through(items, waiting=None):
        for item in items:
            if len(item) == 1:
                sums = own_pairs(item[0])
                later = functools.partial(place_own, cell_of(item[0]), item[0], sums)
            else:
                at, j_block, i_block = item
                sums = pairs(j_block, i_block)
                later = functools.partial(place_pairs, at, i_block, sums)
            if waiting is not None:
                waiting()
            waiting = later
        return waiting

    def within(base):
        found = [(base + j,) for j in range(group)]
        for turn in range(1, group // 2 + 1):
            for j in range(group if 2 * turn < group else group // 2):
                found.append((cell_of(jnp.int32(base + j)), base + j, base + (j + turn) % group))
        return found

    def between(j_base, i_base):
        return [
            (cell_of(jnp.int32(j_base + j)), j_base + j, i_base + i)
            for j in range(group)
            for i in range(group)
        ]

    def deliver(source, t, s, may_be_me=False):
        flat = t * n_sample + s
        copy = r_copy(source, flat, t, s, me)
        if not may_be_me:
            copy.start()
            return

        @pl.when(flat != me)
        def _():
            copy.start()

        @pl.when(flat == me)
        def _():
            res_buf[me] = source[...]

    def mirrored(start):
        whole = cell[start:start + part].reshape(half, LANES)
        square = jnp.concatenate([whole, pltpu.roll(whole, half, 1)], axis=0)
        return whole, square.T[:half]

    def settle(start):
        whole, turned = mirrored(start)
        mask = mask_ref[...]
        first = lax.broadcasted_iota(jnp.int32, wide, 1) < half
        fixed = jnp.where(first, 0.5, 1.0)
        full = jnp.where(mask == 1, whole, jnp.where(mask == 2, fixed, turned))
        done[start:start + part] = full.reshape(part, ROWS, LANES)

    def rows_of(blocks):
        waiting = None
        for k in blocks:
            waiting = work_through([(n_sample + low_of(k), k, i) for i in range(part)], waiting)
        waiting()
        for k in blocks:
            s = lax.bitwise_xor(my_s, k)
            deliver(cell.at[n_sample + lax.rem(s, part)], my_side, s)

    def other_rows(turn, carry):
        last = jnp.where(turn < group // 2, n_sample - 2 - 2 * turn, part)
        rows_of((last + 1, last))
        return carry

    lax.fori_loop(0, group, await_t, 0)
    for k in range(group):
        inv_ref[k] = columns_of(k)
    own_copy.wait()
    lax.fori_loop(1, group, await_x, 0)
    for k in range(group):
        prepare(k)
    work_through(within(0))()
    lax.fori_loop(group, part, await_t, 0)
    for k in range(group, part):
        inv_ref[k] = columns_of(k)
    lax.fori_loop(group, part, await_x, 0)
    for k in range(group, part):
        prepare(k)
    work_through(within(group) + between(group, 0))()
    settle(0)
    for k in range(part - 1, -1, -1):
        s = lax.bitwise_xor(my_s, k)
        deliver(done.at[lax.rem(s, part)], my_side, s, k == 0)
    lax.fori_loop(part, n_sample, await_t, 0)
    for k in range(part, n_sample):
        inv_ref[k] = columns_of(k)
    for k in early:
        await_x(k, 0)
    for k in early:
        prepare(k)
    rows_of(early)
    lax.fori_loop(part, part + group - 2, await_x, 0)
    for k in range(part, part + group - 2):
        prepare(k)
    work_through(within(part))()
    lax.fori_loop(part + group, n_sample, await_x, 0)
    for k in range(part + group, n_sample):
        prepare(k)
    work_through(within(part + group) + between(part + group, part))()
    settle(part)
    for k in range(n_sample - 1, part - 1, -1):
        s = lax.bitwise_xor(my_s, k)
        deliver(done.at[part + lax.rem(s, part)], 1 - my_side, s)
    lax.fori_loop(0, group // 2 + 1, other_rows, 0)
    done[n_sample:n_sample + part] = mirrored(n_sample)[1].reshape(part, ROWS, LANES)
    for k in range(part - 1, -1, -1):
        s = lax.bitwise_xor(my_s, k)
        deliver(done.at[n_sample + lax.rem(s, part)], 1 - my_side, s, k == 0)

    def await_r(k, carry):
        flat, t, s = peer_at(k)
        r_copy(done.at[0], flat, t, s, flat).wait()
        return carry

    lax.fori_loop(1, n_dev, await_r, 0)
    parts = [res_buf[k] for k in range(n_dev)]
    while len(parts) > 1:
        parts = [x + y for x, y in zip(parts[::2], parts[1::2])]
    out_ref[...] = parts[0]


def kernel_body(axes, n_branch, n_sample, abundance, length_table, branch_rows):
    width = abundance.shape[1]
    chunk = width // n_sample
    depth = chunk // LANES
    n_dev = n_branch * n_sample
    half = n_sample * ROWS // n_branch
    sums = pl.pallas_call(
        functools.partial(kernel, axes, n_branch, n_sample, chunk),
        out_shape=pltpu.VMEM((ROWS, LANES), F32),
        in_specs=[pl.BlockSpec(memory_space=pl.ANY)] * 3,
        out_specs=pl.BlockSpec(memory_space=pltpu.VMEM),
        scratch_shapes=[
            pltpu.VMEM((ROWS, width), jnp.bfloat16),
            pltpu.VMEM((width // LANES, LANES), F32),
            pltpu.VMEM((depth, LANES), jnp.int32),
            pltpu.VMEM((n_sample, ROWS, chunk), jnp.bfloat16),
            pltpu.VMEM((1, LANES), F32),
            pltpu.VMEM((n_dev, 1, LANES), F32),
            pltpu.VMEM((n_sample, ROWS, LANES), F32),
            pltpu.VMEM((n_sample, depth, ROWS, LANES), F32),
            pltpu.VMEM((depth, LANES), F32),
            pltpu.VMEM((half, LANES), jnp.int32),
            pltpu.VMEM((n_sample + half // ROWS, ROWS, LANES), F32),
            pltpu.VMEM((n_sample + half // ROWS, ROWS, LANES), F32),
            pltpu.VMEM((n_dev, ROWS, LANES), F32),
            pltpu.SemaphoreType.DMA((3,)),
            pltpu.SemaphoreType.DMA,
            pltpu.SemaphoreType.DMA((n_sample,)),
            pltpu.SemaphoreType.DMA((n_sample,)),
            pltpu.SemaphoreType.DMA((n_dev,)),
            pltpu.SemaphoreType.DMA((n_dev,)),
            pltpu.SemaphoreType.DMA((n_dev,)),
            pltpu.SemaphoreType.DMA((n_dev,)),
        ],
        compiler_params=pltpu.CompilerParams(collective_id=0, has_side_effects=True),
    )(
        abundance,
        length_table.reshape(width // LANES, LANES),
        branch_rows.reshape(n_sample, depth, LANES),
    )
    big, den = sums[:, :half], sums[:, half:2 * half]
    return (2.0 * big - den) / den


def solution(mesh):
    n_branch, n_sample = mesh.shape["branch"], mesh.shape["sample"]
    axes = tuple(mesh.axis_names)

    def body(abundance, length_table, branch_rows):
        rows, width = abundance.shape
        fits = (
            rows == ROWS
            and n_sample * ROWS == LANES
            and n_branch == 2
            and width % (n_sample * ROWS * LANES) == 0
        )
        if not fits:
            return plain_body(abundance, length_table, branch_rows)
        return kernel_body(axes, n_branch, n_sample, abundance, length_table, branch_rows)

    placed = (P("sample", "branch"), P("branch"), P("branch"))
    return jax.shard_map(
        body, mesh=mesh, in_specs=placed, out_specs=P("sample", "branch"), check_vma=False
    )
```

```python
import functools

import jax
import jax.numpy as jnp
from jax import lax
from jax.experimental import pallas as pl
from jax.experimental.pallas import tpu as pltpu
from jax.sharding import PartitionSpec as P

MESH = pl.DeviceIdType.MESH
F32 = jnp.float32
ROWS = 8
LANES = 128


def pair_sums(mine, other, lengths):
    count, width = mine.shape
    others = other.shape[0]
    block_size = width
    while block_size > 512 and block_size % 2 == 0 and (block_size * count * others > 2097152):
        block_size = block_size // 2
    block_count = width // block_size

    def absorb(carry, turn):
        begin = turn * block_size
        left = lax.dynamic_slice_in_dim(mine, begin, block_size, 1).astype(F32)[:, None, :]
        right = lax.dynamic_slice_in_dim(other, begin, block_size, 1).astype(F32)[None, :, :]
        weight = lax.dynamic_slice_in_dim(lengths, begin, block_size, 0)[None, None, :]
        summed = left + right
        inverse = lax.rsqrt(summed)
        return (
            (
                carry[0] + jnp.sum(weight * jnp.abs(left - right) * inverse, axis=2),
                carry[1] + jnp.sum(weight * summed * inverse, axis=2),
            ),
            None,
        )

    empty = jnp.zeros((count, others), F32)
    result, unused = lax.scan(absorb, (empty, empty), jnp.arange(block_count, dtype=jnp.int32))
    return result


def plain_body(abundance, length_table, branch_rows):
    values = abundance.astype(F32)
    totals = lax.psum(jnp.sum(values, axis=1), "branch")
    shares = (values / totals[:, None]).astype(jnp.bfloat16)
    lengths = jnp.take(length_table, branch_rows)
    numer_part, denom_part = pair_sums(
        shares, lax.all_gather(shares, "sample", axis=0, tiled=True), lengths
    )
    summed = (
        lax.psum_scatter(numer_part, "branch", scatter_dimension=1, tiled=True),
        lax.psum_scatter(denom_part, "branch", scatter_dimension=1, tiled=True),
    )
    return summed[0] / summed[1]


def kernel(
    axes, n_branch, n_sample, chunk,
    ab_hbm, table_hbm, rows_hbm, out_ref,
    ab, table, rows, x_buf, tot_send, tot_buf, inv_ref, p_ref, l2_ref, mask_ref, cell, done, res_buf,
    local_sem, own_sem, x_send_sem, x_recv_sem, t_send_sem, t_recv_sem, r_send_sem, r_recv_sem,
):
    n_dev = n_branch * n_sample
    depth = chunk // LANES
    part = n_sample // n_branch
    half = part * ROWS
    group = part // 2
    my_t = lax.axis_index("branch")
    my_s = lax.axis_index("sample")
    me = my_t * n_sample + my_s
    my_side, my_low = my_s // part, lax.rem(my_s, part)

    def place(t, s):
        where = {"branch": t, "sample": s}
        return tuple(where[name] for name in axes)

    def peer_at(k):
        flat = lax.bitwise_xor(me, k)
        return flat, flat // n_sample, lax.rem(flat, n_sample)

    barrier = pltpu.get_barrier_semaphore()

    def greet(k, carry):
        flat, t, s = peer_at(n_dev - k)
        pl.semaphore_signal(barrier, inc=1, device_id=place(t, s), device_id_type=MESH)
        return carry

    ab_copy = pltpu.make_async_copy(ab_hbm, ab, local_sem.at[0])
    table_copy = pltpu.make_async_copy(table_hbm, table, local_sem.at[1])
    rows_copy = pltpu.make_async_copy(rows_hbm.at[my_s], rows, local_sem.at[2])
    own_copy = pltpu.make_async_copy(
        ab_hbm.at[:, pl.ds(pl.multiple_of(my_s * chunk, chunk), chunk)], x_buf.at[my_s], own_sem
    )
    ab_copy.start()
    lax.fori_loop(1, n_dev, greet, 0)
    table_copy.start()
    rows_copy.start()
    own_copy.start()

    def x_copy(to_s, slot, recv):
        return pltpu.make_async_remote_copy(
            src_ref=ab_hbm.at[:, pl.ds(pl.multiple_of(to_s * chunk, chunk), chunk)],
            dst_ref=x_buf.at[slot],
            send_sem=x_send_sem.at[to_s],
            recv_sem=x_recv_sem.at[recv],
            device_id=place(my_t, to_s),
            device_id_type=MESH,
        )

    def t_copy(flat, t, s, slot):
        return pltpu.make_async_remote_copy(
            src_ref=tot_send,
            dst_ref=tot_buf.at[slot],
            send_sem=t_send_sem.at[flat],
            recv_sem=t_recv_sem.at[slot],
            device_id=place(t, s),
            device_id_type=MESH,
        )

    def r_copy(source, flat, t, s, slot):
        return pltpu.make_async_remote_copy(
            src_ref=source,
            dst_ref=res_buf.at[slot],
            send_sem=r_send_sem.at[flat],
            recv_sem=r_recv_sem.at[slot],
            device_id=place(t, s),
            device_id_type=MESH,
        )

    lane = lax.broadcasted_iota(jnp.int32, (ROWS, LANES), 1)
    sub = lax.broadcasted_iota(jnp.int32, (ROWS, LANES), 0)
    eye = lane == sub
    column = lane % half
    is_numer = lane < half

    cell[...] = jnp.zeros_like(cell)
    ab_copy.wait()
    step = min(chunk, 1024)

    def add_up(turn, acc):
        return acc + ab[:, pl.ds(pl.multiple_of(turn * step, step), step)].astype(F32)

    acc = lax.fori_loop(0, n_sample * chunk // step, add_up, jnp.zeros((ROWS, step), F32))
    total = jnp.sum(acc, axis=1, keepdims=True)
    line = jnp.sum(jnp.where(eye, total, 0.0), axis=0, keepdims=True)
    tot_send[...] = line
    tot_buf[me] = line

    pl.semaphore_wait(barrier, n_dev - 1)

    def send_t(k):
        flat, t, s = peer_at(k)
        t_copy(flat, t, s, me).start()

    def send_x(k):
        x_copy(lax.bitwise_xor(my_s, k), my_s, my_s).start()

    send_t(n_sample)
    for k in range(1, part):
        send_t(k)
        send_t(n_sample + k)
        if k < group:
            send_x(k)
    for k in range(group, part):
        send_x(k)
    for k in range(part, n_sample):
        send_t(k)
        send_t(n_sample + k)
    early = (part + group - 2, part + group - 1)
    for k in (*early, *range(part, part + group - 2)):
        send_x(k)
    for k in range(part + group, n_sample):
        send_x(k)

    table_copy.wait()
    rows_copy.wait()
    index = rows[...]
    high, low = index // LANES, index % LANES

    def look_up(h, found):
        line = jnp.broadcast_to(table[pl.ds(h, 1), :], (depth, LANES))
        picked = jnp.take_along_axis(line, low, axis=1, mode="promise_in_bounds")
        return jnp.where(high == h, picked, found)

    lengths = lax.fori_loop(
        0, table.shape[0], look_up, jnp.zeros((depth, LANES), F32), unroll=8
    )
    l2_ref[...] = lengths * lengths

    wide = (half, LANES)
    row_at = lax.broadcasted_iota(jnp.int32, wide, 0)
    column_at = lax.broadcasted_iota(jnp.int32, wide, 1) % half
    row_block = lax.bitwise_xor(row_at // ROWS, my_low)
    column_block = lax.bitwise_xor(column_at // ROWS, my_low)
    apart = (column_block - row_block + part) % group
    turned = (2 * apart < group) | ((2 * apart == group) & (2 * (row_block % group) < group))
    inside = (row_at - column_at + half) % ROWS
    same = row_block == column_block
    row_half, column_half = row_block // group, column_block // group
    direct = (
        (same & (2 * inside <= ROWS))
        | (~same & (row_half == column_half) & turned)
        | (row_half > column_half)
    )
    mask_ref[...] = jnp.where(same & (inside == 0), 2, jnp.where(direct, 1, 0))

    def columns_of(k):
        s = lax.bitwise_xor(my_s, k)
        total = tot_buf[s]
        for t in range(1, n_branch):
            total = total + tot_buf[t * n_sample + s]
        spread = jnp.where(eye, jnp.broadcast_to(total, (ROWS, LANES)), 0.0)
        return 1.0 / jnp.broadcast_to(jnp.sum(spread, axis=1, keepdims=True), (ROWS, LANES))

    def await_t(k, carry):
        s = lax.bitwise_xor(my_s, k)
        for t in range(n_branch):
            flat = t * n_sample + s

            @pl.when(flat != me)
            def _():
                t_copy(flat, t, s, flat).wait()

        return carry

    def await_x(k, carry):
        s = lax.bitwise_xor(my_s, k)
        x_copy(s, s, s).wait()
        return carry

    def prepare(k):
        s = lax.bitwise_xor(my_s, k)
        inverse = inv_ref[k]
        for r in range(depth):
            values = x_buf[s, :, r * LANES:(r + 1) * LANES].astype(F32)
            shares = (values * inverse).astype(jnp.bfloat16).astype(F32)
            p_ref[k, r] = shares * l2_ref[r:r + 1, :]

    def low_of(k):
        return lax.bitwise_xor(my_low, lax.rem(k, part))

    def terms(p, q):
        summed = p + q
        inverse = lax.rsqrt(summed)
        return jnp.maximum(p, q) * inverse, summed * inverse

    def gather(pieces):
        top, bottom = pieces[0]
        for more_top, more_bottom in pieces[1:]:
            top, bottom = top + more_top, bottom + more_bottom
        return top, bottom

    def pairs(j_block, i_block):
        others = [p_ref[j_block, r] for r in range(depth)]
        sums = []
        for i in range(ROWS):
            sums += gather(
                [terms(p_ref[i_block, r, pl.ds(i, 1), :], others[r]) for r in range(depth)]
            )
        return tuple(sums)

    def place_pairs(at, i_block, sums):
        new = jnp.zeros((ROWS, LANES), F32)
        for i in range(ROWS):
            top = jnp.sum(sums[2 * i], axis=1, keepdims=True)
            bottom = jnp.sum(sums[2 * i + 1], axis=1, keepdims=True)
            new = jnp.where(column % ROWS == i, jnp.where(is_numer, top, bottom), new)
        cell[at] = jnp.where(column // ROWS == low_of(i_block), new, cell[at])

    def own_pairs(block):
        mine = [p_ref[block, r] for r in range(depth)]
        sums = []
        for turn in range(1, ROWS // 2 + 1):
            sums += gather([terms(pltpu.roll(q, turn, 0), q) for q in mine])
        return tuple(sums)

    def place_own(at, block, sums):
        base = low_of(block) * ROWS
        now = cell[at]
        for turn in range(1, ROWS // 2 + 1):
            top = jnp.sum(sums[2 * turn - 2], axis=1, keepdims=True)
            bottom = jnp.sum(sums[2 * turn - 1], axis=1, keepdims=True)
            here = column - base == (sub + ROWS - turn) % ROWS
            now = jnp.where(here, jnp.where(is_numer, top, bottom), now)
        cell[at] = now

    def cell_of(k):
        return (k // part) * part + low_of(k)

    def work_through(items, waiting=None):
        for item in items:
            if len(item) == 1:
                sums = own_pairs(item[0])
                later = functools.partial(place_own, cell_of(item[0]), item[0], sums)
            else:
                at, j_block, i_block = item
                sums = pairs(j_block, i_block)
                later = functools.partial(place_pairs, at, i_block, sums)
            if waiting is not None:
                waiting()
            waiting = later
        return waiting

    def within(base):
        found = [(base + j,) for j in range(group)]
        for turn in range(1, group // 2 + 1):
            for j in range(group if 2 * turn < group else group // 2):
                found.append((cell_of(jnp.int32(base + j)), base + j, base + (j + turn) % group))
        return found

    def between(j_base, i_base):
        return [
            (cell_of(jnp.int32(j_base + j)), j_base + j, i_base + i)
            for j in range(group)
            for i in range(group)
        ]

    def deliver(source, t, s, may_be_me=False):
        flat = t * n_sample + s
        copy = r_copy(source, flat, t, s, me)
        if not may_be_me:
            copy.start()
            return

        @pl.when(flat != me)
        def _():
            copy.start()

        @pl.when(flat == me)
        def _():
            res_buf[me] = source[...]

    def mirrored(start):
        whole = cell[start:start + part].reshape(half, LANES)
        square = jnp.concatenate([whole, pltpu.roll(whole, half, 1)], axis=0)
        return whole, square.T[:half]

    def settle(start):
        whole, turned = mirrored(start)
        mask = mask_ref[...]
        first = lax.broadcasted_iota(jnp.int32, wide, 1) < half
        fixed = jnp.where(first, 0.5, 1.0)
        full = jnp.where(mask == 1, whole, jnp.where(mask == 2, fixed, turned))
        done[start:start + part] = full.reshape(part, ROWS, LANES)

    def rows_of(blocks):
        waiting = None
        for k in blocks:
            waiting = work_through([(n_sample + low_of(k), k, i) for i in range(part)], waiting)
        waiting()
        for k in blocks:
            s = lax.bitwise_xor(my_s, k)
            deliver(cell.at[n_sample + lax.rem(s, part)], my_side, s)

    def other_rows(turn, carry):
        last = jnp.where(turn < group // 2, n_sample - 2 - 2 * turn, part)
        rows_of((last + 1, last))
        return carry

    lax.fori_loop(0, group, await_t, 0)
    for k in range(group):
        inv_ref[k] = columns_of(k)
    own_copy.wait()
    lax.fori_loop(1, group, await_x, 0)
    for k in range(group):
        prepare(k)
    work_through(within(0))()
    lax.fori_loop(group, part, await_t, 0)
    for k in range(group, part):
        inv_ref[k] = columns_of(k)
    lax.fori_loop(group, part, await_x, 0)
    for k in range(group, part):
        prepare(k)
    work_through(within(group) + between(group, 0))()
    lax.fori_loop(part, n_sample, await_t, 0)
    for k in range(part, n_sample):
        inv_ref[k] = columns_of(k)
    for k in early:
        await_x(k, 0)
    for k in early:
        prepare(k)
    settle(0)
    rows_of(early)
    for k in range(part - 1, -1, -1):
        s = lax.bitwise_xor(my_s, k)
        deliver(done.at[lax.rem(s, part)], my_side, s, k == 0)
    lax.fori_loop(part, part + group - 2, await_x, 0)
    for k in range(part, part + group - 2):
        prepare(k)
    work_through(within(part))()
    lax.fori_loop(part + group, n_sample, await_x, 0)
    for k in range(part + group, n_sample):
        prepare(k)
    work_through(within(part + group) + between(part + group, part))()
    settle(part)
    for k in range(n_sample - 1, part - 1, -1):
        s = lax.bitwise_xor(my_s, k)
        deliver(done.at[part + lax.rem(s, part)], 1 - my_side, s)
    lax.fori_loop(0, group // 2 + 1, other_rows, 0)
    done[n_sample:n_sample + part] = mirrored(n_sample)[1].reshape(part, ROWS, LANES)
    for k in range(part - 1, -1, -1):
        s = lax.bitwise_xor(my_s, k)
        deliver(done.at[n_sample + lax.rem(s, part)], 1 - my_side, s, k == 0)

    def await_r(k, carry):
        flat, t, s = peer_at(k)
        r_copy(done.at[0], flat, t, s, flat).wait()
        return carry

    lax.fori_loop(1, n_dev, await_r, 0)
    parts = [res_buf[k] for k in range(n_dev)]
    while len(parts) > 1:
        parts = [x + y for x, y in zip(parts[::2], parts[1::2])]
    out_ref[...] = parts[0]


def kernel_body(axes, n_branch, n_sample, abundance, length_table, branch_rows):
    width = abundance.shape[1]
    chunk = width // n_sample
    depth = chunk // LANES
    n_dev = n_branch * n_sample
    half = n_sample * ROWS // n_branch
    sums = pl.pallas_call(
        functools.partial(kernel, axes, n_branch, n_sample, chunk),
        out_shape=pltpu.VMEM((ROWS, LANES), F32),
        in_specs=[pl.BlockSpec(memory_space=pl.ANY)] * 3,
        out_specs=pl.BlockSpec(memory_space=pltpu.VMEM),
        scratch_shapes=[
            pltpu.VMEM((ROWS, width), jnp.bfloat16),
            pltpu.VMEM((width // LANES, LANES), F32),
            pltpu.VMEM((depth, LANES), jnp.int32),
            pltpu.VMEM((n_sample, ROWS, chunk), jnp.bfloat16),
            pltpu.VMEM((1, LANES), F32),
            pltpu.VMEM((n_dev, 1, LANES), F32),
            pltpu.VMEM((n_sample, ROWS, LANES), F32),
            pltpu.VMEM((n_sample, depth, ROWS, LANES), F32),
            pltpu.VMEM((depth, LANES), F32),
            pltpu.VMEM((half, LANES), jnp.int32),
            pltpu.VMEM((n_sample + half // ROWS, ROWS, LANES), F32),
            pltpu.VMEM((n_sample + half // ROWS, ROWS, LANES), F32),
            pltpu.VMEM((n_dev, ROWS, LANES), F32),
            pltpu.SemaphoreType.DMA((3,)),
            pltpu.SemaphoreType.DMA,
            pltpu.SemaphoreType.DMA((n_sample,)),
            pltpu.SemaphoreType.DMA((n_sample,)),
            pltpu.SemaphoreType.DMA((n_dev,)),
            pltpu.SemaphoreType.DMA((n_dev,)),
            pltpu.SemaphoreType.DMA((n_dev,)),
            pltpu.SemaphoreType.DMA((n_dev,)),
        ],
        compiler_params=pltpu.CompilerParams(collective_id=0, has_side_effects=True),
    )(
        abundance,
        length_table.reshape(width // LANES, LANES),
        branch_rows.reshape(n_sample, depth, LANES),
    )
    big, den = sums[:, :half], sums[:, half:2 * half]
    return (2.0 * big - den) / den


def solution(mesh):
    n_branch, n_sample = mesh.shape["branch"], mesh.shape["sample"]
    axes = tuple(mesh.axis_names)

    def body(abundance, length_table, branch_rows):
        rows, width = abundance.shape
        fits = (
            rows == ROWS
            and n_sample * ROWS == LANES
            and n_branch == 2
            and width % (n_sample * ROWS * LANES) == 0
        )
        if not fits:
            return plain_body(abundance, length_table, branch_rows)
        return kernel_body(axes, n_branch, n_sample, abundance, length_table, branch_rows)

    placed = (P("sample", "branch"), P("branch"), P("branch"))
    return jax.shard_map(
        body, mesh=mesh, in_specs=placed, out_specs=P("sample", "branch"), check_vma=False
    )
```

```python
import functools

import jax
import jax.numpy as jnp
from jax import lax
from jax.experimental import pallas as pl
from jax.experimental.pallas import tpu as pltpu
from jax.sharding import PartitionSpec as P

MESH = pl.DeviceIdType.MESH
F32 = jnp.float32
ROWS = 8
LANES = 128


def pair_sums(mine, other, lengths):
    count, width = mine.shape
    others = other.shape[0]
    block_size = width
    while block_size > 512 and block_size % 2 == 0 and (block_size * count * others > 2097152):
        block_size = block_size // 2
    block_count = width // block_size

    def absorb(carry, turn):
        begin = turn * block_size
        left = lax.dynamic_slice_in_dim(mine, begin, block_size, 1).astype(F32)[:, None, :]
        right = lax.dynamic_slice_in_dim(other, begin, block_size, 1).astype(F32)[None, :, :]
        weight = lax.dynamic_slice_in_dim(lengths, begin, block_size, 0)[None, None, :]
        summed = left + right
        inverse = lax.rsqrt(summed)
        return (
            (
                carry[0] + jnp.sum(weight * jnp.abs(left - right) * inverse, axis=2),
                carry[1] + jnp.sum(weight * summed * inverse, axis=2),
            ),
            None,
        )

    empty = jnp.zeros((count, others), F32)
    result, unused = lax.scan(absorb, (empty, empty), jnp.arange(block_count, dtype=jnp.int32))
    return result


def plain_body(abundance, length_table, branch_rows):
    values = abundance.astype(F32)
    totals = lax.psum(jnp.sum(values, axis=1), "branch")
    shares = (values / totals[:, None]).astype(jnp.bfloat16)
    lengths = jnp.take(length_table, branch_rows)
    numer_part, denom_part = pair_sums(
        shares, lax.all_gather(shares, "sample", axis=0, tiled=True), lengths
    )
    summed = (
        lax.psum_scatter(numer_part, "branch", scatter_dimension=1, tiled=True),
        lax.psum_scatter(denom_part, "branch", scatter_dimension=1, tiled=True),
    )
    return summed[0] / summed[1]


def kernel(
    axes, n_branch, n_sample, chunk,
    ab_hbm, table_hbm, rows_hbm, out_ref,
    ab, table, rows, x_buf, tot_send, tot_buf, inv_ref, p_ref, l2_ref, mask_ref, cell, done, res_buf,
    local_sem, own_sem, x_send_sem, x_recv_sem, t_send_sem, t_recv_sem, r_send_sem, r_recv_sem,
):
    n_dev = n_branch * n_sample
    depth = chunk // LANES
    part = n_sample // n_branch
    half = part * ROWS
    group = part // 2
    my_t = lax.axis_index("branch")
    my_s = lax.axis_index("sample")
    me = my_t * n_sample + my_s
    my_side, my_low = my_s // part, lax.rem(my_s, part)

    def place(t, s):
        where = {"branch": t, "sample": s}
        return tuple(where[name] for name in axes)

    def peer_at(k):
        flat = lax.bitwise_xor(me, k)
        return flat, flat // n_sample, lax.rem(flat, n_sample)

    barrier = pltpu.get_barrier_semaphore()

    def greet(k, carry):
        flat, t, s = peer_at(n_dev - k)
        pl.semaphore_signal(barrier, inc=1, device_id=place(t, s), device_id_type=MESH)
        return carry

    ab_copy = pltpu.make_async_copy(ab_hbm, ab, local_sem.at[0])
    table_copy = pltpu.make_async_copy(table_hbm, table, local_sem.at[1])
    rows_copy = pltpu.make_async_copy(rows_hbm.at[my_s], rows, local_sem.at[2])
    own_copy = pltpu.make_async_copy(
        ab_hbm.at[:, pl.ds(pl.multiple_of(my_s * chunk, chunk), chunk)], x_buf.at[my_s], own_sem
    )
    ab_copy.start()
    for k in range(1, n_dev):
        greet(k, 0)
    table_copy.start()
    rows_copy.start()
    own_copy.start()

    def x_copy(to_s, slot, recv):
        return pltpu.make_async_remote_copy(
            src_ref=ab_hbm.at[:, pl.ds(pl.multiple_of(to_s * chunk, chunk), chunk)],
            dst_ref=x_buf.at[slot],
            send_sem=x_send_sem.at[to_s],
            recv_sem=x_recv_sem.at[recv],
            device_id=place(my_t, to_s),
            device_id_type=MESH,
        )

    def t_copy(flat, t, s, slot):
        return pltpu.make_async_remote_copy(
            src_ref=tot_send,
            dst_ref=tot_buf.at[slot],
            send_sem=t_send_sem.at[flat],
            recv_sem=t_recv_sem.at[slot],
            device_id=place(t, s),
            device_id_type=MESH,
        )

    def r_copy(source, flat, t, s, slot):
        return pltpu.make_async_remote_copy(
            src_ref=source,
            dst_ref=res_buf.at[slot],
            send_sem=r_send_sem.at[flat],
            recv_sem=r_recv_sem.at[slot],
            device_id=place(t, s),
            device_id_type=MESH,
        )

    lane = lax.broadcasted_iota(jnp.int32, (ROWS, LANES), 1)
    sub = lax.broadcasted_iota(jnp.int32, (ROWS, LANES), 0)
    eye = lane == sub
    column = lane % half
    is_numer = lane < half

    cell[...] = jnp.zeros_like(cell)
    ab_copy.wait()
    step = min(chunk, 1024)

    def add_up(turn, acc):
        return acc + ab[:, pl.ds(pl.multiple_of(turn * step, step), step)].astype(F32)

    acc = lax.fori_loop(0, n_sample * chunk // step, add_up, jnp.zeros((ROWS, step), F32))
    total = jnp.sum(acc, axis=1, keepdims=True)
    line = jnp.sum(jnp.where(eye, total, 0.0), axis=0, keepdims=True)
    tot_send[...] = line
    tot_buf[me] = line

    pl.semaphore_wait(barrier, n_dev - 1)

    def send_t(k):
        flat, t, s = peer_at(k)
        t_copy(flat, t, s, me).start()

    def send_x(k):
        x_copy(lax.bitwise_xor(my_s, k), my_s, my_s).start()

    send_t(n_sample)
    for k in range(1, part):
        send_t(k)
        send_t(n_sample + k)
        if k < group:
            send_x(k)
    for k in range(group, part):
        send_x(k)
    for k in range(part, n_sample):
        send_t(k)
        send_t(n_sample + k)
    early = (part + group - 2, part + group - 1)
    for k in (*early, *range(part, part + group - 2)):
        send_x(k)
    for k in range(part + group, n_sample):
        send_x(k)

    table_copy.wait()
    rows_copy.wait()
    index = rows[...]
    high, low = index // LANES, index % LANES

    def look_up(h, found):
        line = jnp.broadcast_to(table[pl.ds(h, 1), :], (depth, LANES))
        picked = jnp.take_along_axis(line, low, axis=1, mode="promise_in_bounds")
        return jnp.where(high == h, picked, found)

    lengths = lax.fori_loop(
        0, table.shape[0], look_up, jnp.zeros((depth, LANES), F32), unroll=8
    )
    l2_ref[...] = lengths * lengths

    wide = (half, LANES)
    row_at = lax.broadcasted_iota(jnp.int32, wide, 0)
    column_at = lax.broadcasted_iota(jnp.int32, wide, 1) % half
    row_block = lax.bitwise_xor(row_at // ROWS, my_low)
    column_block = lax.bitwise_xor(column_at // ROWS, my_low)
    apart = (column_block - row_block + part) % group
    turned = (2 * apart < group) | ((2 * apart == group) & (2 * (row_block % group) < group))
    inside = (row_at - column_at + half) % ROWS
    same = row_block == column_block
    row_half, column_half = row_block // group, column_block // group
    direct = (
        (same & (2 * inside <= ROWS))
        | (~same & (row_half == column_half) & turned)
        | (row_half > column_half)
    )
    mask_ref[...] = jnp.where(same & (inside == 0), 2, jnp.where(direct, 1, 0))

    def columns_of(k):
        s = lax.bitwise_xor(my_s, k)
        total = tot_buf[s]
        for t in range(1, n_branch):
            total = total + tot_buf[t * n_sample + s]
        spread = jnp.where(eye, jnp.broadcast_to(total, (ROWS, LANES)), 0.0)
        return 1.0 / jnp.broadcast_to(jnp.sum(spread, axis=1, keepdims=True), (ROWS, LANES))

    def await_t(k, carry):
        s = lax.bitwise_xor(my_s, k)
        for t in range(n_branch):
            flat = t * n_sample + s

            @pl.when(flat != me)
            def _():
                t_copy(flat, t, s, flat).wait()

        return carry

    def await_x(k, carry):
        s = lax.bitwise_xor(my_s, k)
        x_copy(s, s, s).wait()
        return carry

    def prepare(k):
        s = lax.bitwise_xor(my_s, k)
        inverse = inv_ref[k]
        for r in range(depth):
            values = x_buf[s, :, r * LANES:(r + 1) * LANES].astype(F32)
            shares = (values * inverse).astype(jnp.bfloat16).astype(F32)
            p_ref[k, r] = shares * l2_ref[r:r + 1, :]

    def low_of(k):
        return lax.bitwise_xor(my_low, lax.rem(k, part))

    def terms(p, q):
        summed = p + q
        inverse = lax.rsqrt(summed)
        return jnp.maximum(p, q) * inverse, summed * inverse

    def gather(pieces):
        top, bottom = pieces[0]
        for more_top, more_bottom in pieces[1:]:
            top, bottom = top + more_top, bottom + more_bottom
        return top, bottom

    def pairs(j_block, i_block):
        others = [p_ref[j_block, r] for r in range(depth)]
        sums = []
        for i in range(ROWS):
            sums += gather(
                [terms(p_ref[i_block, r, pl.ds(i, 1), :], others[r]) for r in range(depth)]
            )
        return tuple(sums)

    def place_pairs(at, i_block, sums):
        new = jnp.zeros((ROWS, LANES), F32)
        for i in range(ROWS):
            top = jnp.sum(sums[2 * i], axis=1, keepdims=True)
            bottom = jnp.sum(sums[2 * i + 1], axis=1, keepdims=True)
            new = jnp.where(column % ROWS == i, jnp.where(is_numer, top, bottom), new)
        cell[at] = jnp.where(column // ROWS == low_of(i_block), new, cell[at])

    def own_pairs(block):
        mine = [p_ref[block, r] for r in range(depth)]
        sums = []
        for turn in range(1, ROWS // 2 + 1):
            sums += gather([terms(pltpu.roll(q, turn, 0), q) for q in mine])
        return tuple(sums)

    def place_own(at, block, sums):
        base = low_of(block) * ROWS
        now = cell[at]
        for turn in range(1, ROWS // 2 + 1):
            top = jnp.sum(sums[2 * turn - 2], axis=1, keepdims=True)
            bottom = jnp.sum(sums[2 * turn - 1], axis=1, keepdims=True)
            here = column - base == (sub + ROWS - turn) % ROWS
            now = jnp.where(here, jnp.where(is_numer, top, bottom), now)
        cell[at] = now

    def cell_of(k):
        return (k // part) * part + low_of(k)

    def work_through(items, waiting=None):
        for item in items:
            if len(item) == 1:
                sums = own_pairs(item[0])
                later = functools.partial(place_own, cell_of(item[0]), item[0], sums)
            else:
                at, j_block, i_block = item
                sums = pairs(j_block, i_block)
                later = functools.partial(place_pairs, at, i_block, sums)
            if waiting is not None:
                waiting()
            waiting = later
        return waiting

    def within(base):
        found = [(base + j,) for j in range(group)]
        for turn in range(1, group // 2 + 1):
            for j in range(group if 2 * turn < group else group // 2):
                found.append((cell_of(jnp.int32(base + j)), base + j, base + (j + turn) % group))
        return found

    def between(j_base, i_base):
        return [
            (cell_of(jnp.int32(j_base + j)), j_base + j, i_base + i)
            for j in range(group)
            for i in range(group)
        ]

    def deliver(source, t, s, may_be_me=False):
        flat = t * n_sample + s
        copy = r_copy(source, flat, t, s, me)
        if not may_be_me:
            copy.start()
            return

        @pl.when(flat != me)
        def _():
            copy.start()

        @pl.when(flat == me)
        def _():
            res_buf[me] = source[...]

    def mirrored(start):
        whole = cell[start:start + part].reshape(half, LANES)
        square = jnp.concatenate([whole, pltpu.roll(whole, half, 1)], axis=0)
        return whole, square.T[:half]

    def settle(start):
        whole, turned = mirrored(start)
        mask = mask_ref[...]
        first = lax.broadcasted_iota(jnp.int32, wide, 1) < half
        fixed = jnp.where(first, 0.5, 1.0)
        full = jnp.where(mask == 1, whole, jnp.where(mask == 2, fixed, turned))
        done[start:start + part] = full.reshape(part, ROWS, LANES)

    def rows_of(blocks):
        waiting = None
        for k in blocks:
            waiting = work_through([(n_sample + low_of(k), k, i) for i in range(part)], waiting)
        waiting()
        for k in blocks:
            s = lax.bitwise_xor(my_s, k)
            deliver(cell.at[n_sample + lax.rem(s, part)], my_side, s)

    def other_rows(turn, carry):
        last = jnp.where(turn < group // 2, n_sample - 2 - 2 * turn, part)
        rows_of((last + 1, last))
        return carry

    lax.fori_loop(0, group, await_t, 0)
    for k in range(group):
        inv_ref[k] = columns_of(k)
    own_copy.wait()
    lax.fori_loop(1, group, await_x, 0)
    for k in range(group):
        prepare(k)
    work_through(within(0))()
    lax.fori_loop(group, part, await_t, 0)
    for k in range(group, part):
        inv_ref[k] = columns_of(k)
    lax.fori_loop(group, part, await_x, 0)
    for k in range(group, part):
        prepare(k)
    work_through(within(group) + between(group, 0))()
    lax.fori_loop(part, n_sample, await_t, 0)
    for k in range(part, n_sample):
        inv_ref[k] = columns_of(k)
    for k in early:
        await_x(k, 0)
    for k in early:
        prepare(k)
    settle(0)
    rows_of(early)
    for k in range(part - 1, -1, -1):
        s = lax.bitwise_xor(my_s, k)
        deliver(done.at[lax.rem(s, part)], my_side, s, k == 0)
    lax.fori_loop(part, part + group - 2, await_x, 0)
    for k in range(part, part + group - 2):
        prepare(k)
    work_through(within(part))()
    lax.fori_loop(part + group, n_sample, await_x, 0)
    for k in range(part + group, n_sample):
        prepare(k)
    work_through(within(part + group) + between(part + group, part))()
    settle(part)
    for k in range(n_sample - 1, part - 1, -1):
        s = lax.bitwise_xor(my_s, k)
        deliver(done.at[part + lax.rem(s, part)], 1 - my_side, s)
    lax.fori_loop(0, group // 2 + 1, other_rows, 0)
    done[n_sample:n_sample + part] = mirrored(n_sample)[1].reshape(part, ROWS, LANES)
    for k in range(part - 1, -1, -1):
        s = lax.bitwise_xor(my_s, k)
        deliver(done.at[n_sample + lax.rem(s, part)], 1 - my_side, s, k == 0)

    def await_r(k, carry):
        flat, t, s = peer_at(k)
        r_copy(done.at[0], flat, t, s, flat).wait()
        return carry

    lax.fori_loop(1, n_dev, await_r, 0)
    parts = [res_buf[k] for k in range(n_dev)]
    while len(parts) > 1:
        parts = [x + y for x, y in zip(parts[::2], parts[1::2])]
    out_ref[...] = parts[0]


def kernel_body(axes, n_branch, n_sample, abundance, length_table, branch_rows):
    width = abundance.shape[1]
    chunk = width // n_sample
    depth = chunk // LANES
    n_dev = n_branch * n_sample
    half = n_sample * ROWS // n_branch
    sums = pl.pallas_call(
        functools.partial(kernel, axes, n_branch, n_sample, chunk),
        out_shape=pltpu.VMEM((ROWS, LANES), F32),
        in_specs=[pl.BlockSpec(memory_space=pl.ANY)] * 3,
        out_specs=pl.BlockSpec(memory_space=pltpu.VMEM),
        scratch_shapes=[
            pltpu.VMEM((ROWS, width), jnp.bfloat16),
            pltpu.VMEM((width // LANES, LANES), F32),
            pltpu.VMEM((depth, LANES), jnp.int32),
            pltpu.VMEM((n_sample, ROWS, chunk), jnp.bfloat16),
            pltpu.VMEM((1, LANES), F32),
            pltpu.VMEM((n_dev, 1, LANES), F32),
            pltpu.VMEM((n_sample, ROWS, LANES), F32),
            pltpu.VMEM((n_sample, depth, ROWS, LANES), F32),
            pltpu.VMEM((depth, LANES), F32),
            pltpu.VMEM((half, LANES), jnp.int32),
            pltpu.VMEM((n_sample + half // ROWS, ROWS, LANES), F32),
            pltpu.VMEM((n_sample + half // ROWS, ROWS, LANES), F32),
            pltpu.VMEM((n_dev, ROWS, LANES), F32),
            pltpu.SemaphoreType.DMA((3,)),
            pltpu.SemaphoreType.DMA,
            pltpu.SemaphoreType.DMA((n_sample,)),
            pltpu.SemaphoreType.DMA((n_sample,)),
            pltpu.SemaphoreType.DMA((n_dev,)),
            pltpu.SemaphoreType.DMA((n_dev,)),
            pltpu.SemaphoreType.DMA((n_dev,)),
            pltpu.SemaphoreType.DMA((n_dev,)),
        ],
        compiler_params=pltpu.CompilerParams(collective_id=0, has_side_effects=True),
    )(
        abundance,
        length_table.reshape(width // LANES, LANES),
        branch_rows.reshape(n_sample, depth, LANES),
    )
    big, den = sums[:, :half], sums[:, half:2 * half]
    return (2.0 * big - den) / den


def solution(mesh):
    n_branch, n_sample = mesh.shape["branch"], mesh.shape["sample"]
    axes = tuple(mesh.axis_names)

    def body(abundance, length_table, branch_rows):
        rows, width = abundance.shape
        fits = (
            rows == ROWS
            and n_sample * ROWS == LANES
            and n_branch == 2
            and width % (n_sample * ROWS * LANES) == 0
        )
        if not fits:
            return plain_body(abundance, length_table, branch_rows)
        return kernel_body(axes, n_branch, n_sample, abundance, length_table, branch_rows)

    placed = (P("sample", "branch"), P("branch"), P("branch"))
    return jax.shard_map(
        body, mesh=mesh, in_specs=placed, out_specs=P("sample", "branch"), check_vma=False
    )
```
